32 devices in a mesh: grp: 2 (over y), seq: 4 (over z), dp: 2 (over x), tp: 2 (over core).
Axes of the slice: x: 2, y: 2, z: 4, core: 2. Of those that a mesh axis runs over, the one named last changes fastest.
Arguments:
- query_image: bfloat16 [4, 1024, 2048], P(('grp', 'dp'), ('seq', 'tp')), parts along dimension 0, may hold values from -8 to 8
- key_image: bfloat16 [4, 1024, 2048], P(('grp', 'dp'), ('seq', 'tp')), parts along dimension 0, may hold values from -8 to 8
- value_image: bfloat16 [4, 1024, 2048], P(('grp', 'dp'), ('seq', 'tp')), parts along dimension 0, may hold values from -6 to 6
- query_text: bfloat16 [4, 128, 2048], P(('grp', 'dp'), ('seq', 'tp')), parts along dimension 0, may hold values from -6 to 6
- key_text: bfloat16 [4, 128, 2048], P(('grp', 'dp'), ('seq', 'tp')), parts along dimension 0, may hold values from -6 to 6
- value_text: bfloat16 [4, 128, 2048], P(('grp', 'dp'), ('seq', 'tp')), parts along dimension 0, may hold values from -6 to 6
- image_query_gain: float32 [128], replicated, may hold values from 1 to 6
- image_key_gain: float32 [128], replicated, may hold values from 1 to 6
- text_query_gain: float32 [128], replicated, may hold values from 1.2 to 2.5
- text_key_gain: float32 [128], replicated, may hold values from 1.2 to 2.5
- text_length: int32 [4], P(('grp', 'dp')), parts along dimension 0, may hold values from 1 to 128
- strata: int32 [4], P(('grp', 'dp')), parts along dimension 0, may hold values from 0 to 63
- image_state: bfloat16 [4, 1024, 3072], P(('grp', 'dp'), ('seq', 'tp')), parts along dimension 0, may hold values from -6 to 6
- target: bfloat16 [4, 1024, 3072], P(('grp', 'dp'), ('seq', 'tp')), parts along dimension 0, may hold values from -6 to 6
- out_weight: bfloat16 [2048, 3072], P('seq', 'tp'), may hold values from -0.125 to 0.125
- gate_table: bfloat16 [64, 3072], replicated, may hold values from -4 to 4
Outputs:
- velocity: bfloat16 [4, 1024, 3072], P(('grp', 'dp'), ('seq', 'tp')), parts along dimension 0
- text_attention: bfloat16 [4, 128, 2048], P(('grp', 'dp'), ('seq', 'tp')), parts along dimension 0
- flow_loss: float32 [2], P('grp'), parts along dimension 0
The draws below stay inside these ranges and needn't reach their ends.
There are 2 independent parts, one for each index of `grp`. The reference program is written for one: setup_inputs(seed, part) draws one part's arguments, and reference() takes and returns one part's arrays. A program takes and returns all parts, laid end to end along the dimension named above; an argument that names none is the same for every part. Nothing has to cross between parts.
Inputs may be any that keep to these rules, and one draw needn't show every extreme that they name: `text_length`: text positions at or beyond a sample's length are padding and are not attended to.
All inputs are finite; a program needn't handle non-finite values.
Results may differ from the reference program's by a relative error of at most 0.012.
The reference program's roundings to bfloat16 on the way count: a program that leaves them out, or rounds other values in their place, can miss the bound.
Values may be sent and summed in bfloat16 or wider, within the bound.
A program may use at most 64 MiB of HBM per device.

```python
import math
import jax
import jax.numpy as jnp
from jax import lax

D = 3072
HEADS = 16
HEAD_DIM = 128
STRATA = 64
SAMPLES = 2
IMG = 1024
TXT = 128
ATTN = 2048


def drawn_pair(key):
    folded = jax.random.fold_in(key, 7331)
    draw_query, draw_key = jax.random.split(folded, 2)
    queries = jnp.clip(jax.random.normal(draw_query, (SAMPLES, IMG, HEADS * HEAD_DIM), jnp.float32), -6.0, 6.0)
    keys_drawn = jnp.clip(jax.random.normal(draw_key, (SAMPLES, IMG, HEADS * HEAD_DIM), jnp.float32), -6.0, 6.0)
    return (queries, keys_drawn)


def draw_query_image(key, part):
    return drawn_pair(key)[0].astype(jnp.bfloat16)


def draw_key_image(key, part):
    return drawn_pair(key)[1].astype(jnp.bfloat16)


def gain_draw(key):
    return jnp.exp(jax.random.uniform(key, (HEAD_DIM,), jnp.float32, jnp.log(1.2), jnp.log(2.5)))


def draw_image_query_gain(key, part):
    return gain_draw(jax.random.fold_in(key, 11))


def draw_image_key_gain(key, part):
    return gain_draw(jax.random.fold_in(key, 13))


def draw_target(key, part):
    folded = jax.random.fold_in(key, 29)
    draw_noise, draw_sample, draw_column = jax.random.split(folded, 3)
    rising = jnp.arange(IMG, dtype=jnp.float32) / IMG
    sample_offset = jax.random.uniform(draw_sample, (SAMPLES,), jnp.float32, -1.0, 1.0)
    column_offset = jnp.clip(0.5 * jax.random.normal(draw_column, (D,), jnp.float32), -1.0, 1.0)
    sample_noise = jnp.clip(jax.random.normal(draw_noise, (SAMPLES, IMG, D), jnp.float32), -2.5, 2.5)
    scaling = 0.5 + rising
    shared = sample_offset[:, None, None] + column_offset[None, None, :]
    return (sample_noise * scaling[None, :, None] + shared).astype(jnp.bfloat16)


def block_scale(own_key, extent, pieces, low, top_value):
    def one(dim, parts):
        draws = jax.random.uniform(jax.random.fold_in(jax.random.fold_in(own_key, 6), dim), (parts,), jnp.float32, low / len(pieces), top_value / len(pieces))
        return jnp.repeat(jnp.exp(draws), extent[dim] // parts).reshape((-1,) + (1,) * (len(extent) - dim - 1))

    gain = one(*pieces[0])
    for cut in pieces[1:]:
        gain = gain * one(*cut)
    return gain


def gaussian(own_key, dims, deviation, reach, pieces=(), kind=jnp.bfloat16):
    gain = block_scale(own_key, dims, pieces, -0.22, 0.18) if pieces else 1.0
    drawn = jax.random.normal(own_key, dims, jnp.float32) * deviation * gain
    return jnp.minimum(jnp.maximum(drawn, -reach), reach).astype(kind)


def setup_inputs(seed: int = 0, part: int = 0) -> dict:
    key_of = jax.random.split(jax.random.key(seed), 17)
    own_keys = jax.random.split(jax.random.fold_in(key_of[16], part), 17)
    query_image = draw_query_image(jax.random.fold_in(jax.random.fold_in(key_of[16], part), 71), part)
    key_image = draw_key_image(jax.random.fold_in(jax.random.fold_in(key_of[16], part), 71), part)
    value_image = gaussian(own_keys[2], (SAMPLES, IMG, ATTN), 1.0, 6.0, ((0, 2), (1, 8)))
    query_text = gaussian(own_keys[3], (SAMPLES, TXT, ATTN), 1.0, 6.0, ((0, 2), (1, 8)))
    key_text = gaussian(own_keys[4], (SAMPLES, TXT, ATTN), 1.0, 6.0, ((0, 2), (1, 8)))
    value_text = gaussian(own_keys[5], (SAMPLES, TXT, ATTN), 1.0, 6.0, ((0, 2), (1, 8)))
    image_query_gain = draw_image_query_gain(jax.random.fold_in(key_of[16], 71), part)
    image_key_gain = draw_image_key_gain(jax.random.fold_in(key_of[16], 71), part)
    text_query_gain = jnp.clip(jnp.exp(jax.random.uniform(key_of[8], (HEAD_DIM,), jnp.float32, math.log(1.2), math.log(2.5))), 1.2, 2.5)
    text_key_gain = jnp.clip(jnp.exp(jax.random.uniform(key_of[9], (HEAD_DIM,), jnp.float32, math.log(1.2), math.log(2.5))), 1.2, 2.5)
    text_length = jax.random.randint(own_keys[10], (SAMPLES,), 1, TXT + 1).astype(jnp.int32)
    strata = jax.random.randint(own_keys[11], (SAMPLES,), 0, STRATA).astype(jnp.int32)
    image_state = gaussian(own_keys[12], (SAMPLES, IMG, D), 1.0, 6.0, ((0, 2), (1, 8)))
    target = draw_target(jax.random.fold_in(jax.random.fold_in(key_of[16], part), 71), part)
    out_weight = gaussian(key_of[14], (ATTN, D), ATTN ** -0.5, 0.125, ((0, 4), (1, 2)))
    gate_table = gaussian(key_of[15], (STRATA, D), 1.0, 4.0)
    return dict(query_image=query_image, key_image=key_image, value_image=value_image, query_text=query_text, key_text=key_text, value_text=value_text, image_query_gain=image_query_gain, image_key_gain=image_key_gain, text_query_gain=text_query_gain, text_key_gain=text_key_gain, text_length=text_length, strata=strata, image_state=image_state, target=target, out_weight=out_weight, gate_table=gate_table)


def head_norm(values, gain_vector):
    columns = values.shape[-1]
    shaped = values.astype(jnp.float32).reshape(values.shape[:-1] + (columns // HEAD_DIM, HEAD_DIM))
    inverse = lax.rsqrt(lax.optimization_barrier(jnp.mean(shaped * shaped, axis=-1, keepdims=True)) + 1e-06)
    return (shaped * inverse * gain_vector).reshape(values.shape).astype(jnp.bfloat16)

def reference(query_image, key_image, value_image, query_text, key_text, value_text, image_query_gain, image_key_gain, text_query_gain, text_key_gain, text_length, strata, image_state, target, out_weight, gate_table):
    queries = jnp.concatenate([head_norm(query_text, text_query_gain), head_norm(query_image, image_query_gain)], axis=1)
    keys_joint = jnp.concatenate([head_norm(key_text, text_key_gain), head_norm(key_image, image_key_gain)], axis=1)
    values_joint = jnp.concatenate([value_text, value_image], axis=1)
    length = TXT + IMG
    positions = jnp.arange(length, dtype=jnp.int32)
    usable = (positions[None, :] >= TXT) | (positions[None, :] < text_length[:, None])

    def single_head(index):
        sample = index // HEADS
        head_start = index % HEADS * HEAD_DIM
        query_block = lax.dynamic_slice_in_dim(queries[sample], head_start, HEAD_DIM, 1)
        key_block = lax.dynamic_slice_in_dim(keys_joint[sample], head_start, HEAD_DIM, 1)
        value_block = lax.dynamic_slice_in_dim(values_joint[sample], head_start, HEAD_DIM, 1)
        scores = jnp.dot(query_block, key_block.T, preferred_element_type=jnp.float32) * HEAD_DIM ** (-0.5)
        scores = jnp.where(usable[sample][None, :], scores, -1e+30)
        row_max = lax.optimization_barrier(jnp.max(scores, axis=1, keepdims=True))
        powers = jnp.exp(scores - row_max)
        weights = (powers / lax.optimization_barrier(jnp.sum(powers, axis=1, keepdims=True))).astype(jnp.bfloat16)
        return jnp.dot(weights, value_block, preferred_element_type=jnp.float32).astype(jnp.bfloat16)
    heads_out = lax.map(single_head, jnp.arange(SAMPLES * HEADS, dtype=jnp.int32))
    attention = heads_out.reshape(SAMPLES, HEADS, length, HEAD_DIM).transpose(0, 2, 1, 3).reshape(SAMPLES, length, HEADS * HEAD_DIM)
    text_attention = attention[:, :TXT]
    image_rows = attention[:, TXT:].reshape(SAMPLES * IMG, HEADS * HEAD_DIM)
    branch = jnp.dot(image_rows, out_weight, preferred_element_type=jnp.float32).reshape(SAMPLES, IMG, D)
    gate_rows = gate_table[strata].astype(jnp.float32)
    combined = image_state.astype(jnp.float32) + gate_rows[:, None, :] * branch
    error_terms = combined - target.astype(jnp.float32)
    flow_loss = (jnp.sum(error_terms * error_terms) / (SAMPLES * IMG * D)).reshape(1)
    return (combined.astype(jnp.bfloat16), text_attention, flow_loss)
```

```python
import functools

import jax
import jax.numpy as jnp
from jax import lax
from jax.experimental import pallas as pl
from jax.experimental.pallas import tpu as pltpu
from jax.sharding import PartitionSpec as P

MESH = pl.DeviceIdType.MESH
VMEM = pl.BlockSpec(memory_space=pltpu.VMEM)
ANY = pl.BlockSpec(memory_space=pl.ANY)
SMALL = 1e-06


def head_norm(values, gain_vector):
    head_dim = gain_vector.shape[0]
    columns = values.shape[-1]
    shaped = values.astype(jnp.float32).reshape(values.shape[:-1] + (columns // head_dim, head_dim))
    inverse = lax.rsqrt(jnp.mean(shaped * shaped, axis=-1, keepdims=True) + 1e-06)
    return (shaped * inverse * gain_vector).reshape(values.shape).astype(jnp.bfloat16)


def attend(query_block, key_split, value_split, usable, factor):
    scores = (
        jnp.einsum("qhd,khd->hqk", query_block, key_split, preferred_element_type=jnp.float32)
        * factor
    )
    scores = jnp.where(usable[None, None, :], scores, -1e30)
    row_max = jnp.max(scores, axis=2, keepdims=True)
    powers = jnp.exp(scores - row_max)
    weights = (powers / jnp.sum(powers, axis=2, keepdims=True)).astype(jnp.bfloat16)
    return jnp.einsum(
        "hqk,khd->qhd", weights, value_split, preferred_element_type=jnp.float32
    ).astype(jnp.bfloat16)


def local(
    query_image,
    key_image,
    value_image,
    query_text,
    key_text,
    value_text,
    image_query_gain,
    image_key_gain,
    text_query_gain,
    text_key_gain,
    text_length,
    strata,
    image_state,
    target,
    out_weight,
    gate_table,
):
    samples = query_image.shape[0]
    image_count = query_image.shape[1]
    text_count = query_text.shape[1]
    local_rows = image_count + text_count
    head_dim = image_query_gain.shape[0]
    seq_count = lax.axis_size("seq")
    core_count = lax.axis_size("tp")
    queries = jnp.concatenate(
        [head_norm(query_text, text_query_gain), head_norm(query_image, image_query_gain)], axis=1
    )
    keys_local = jnp.concatenate(
        [head_norm(key_text, text_key_gain), head_norm(key_image, image_key_gain)], axis=1
    )
    values_local = jnp.concatenate([value_text, value_image], axis=1)
    key_index = jnp.arange(seq_count * core_count * local_rows, dtype=jnp.int32)
    within = key_index % local_rows
    query_heads, key_rows, value_rows = (
        lax.all_to_all(queries, "seq", split_axis=2, concat_axis=1, tiled=True),
        lax.all_to_all(keys_local, "seq", split_axis=2, concat_axis=1, tiled=True),
        lax.all_to_all(values_local, "seq", split_axis=2, concat_axis=1, tiled=True),
    )
    key_heads, value_heads = (
        lax.all_gather(key_rows, "tp", axis=1, tiled=True),
        lax.all_gather(value_rows, "tp", axis=1, tiled=True),
    )
    core_shard = key_index // (seq_count * local_rows)
    seq_shard = key_index // local_rows % seq_count
    text_place = (seq_shard * core_count + core_shard) * text_count + within
    usable = (within[None, :] >= text_count) | (text_place[None, :] < text_length[:, None])
    query_total = query_heads.shape[1]
    heads_device = query_heads.shape[2] // head_dim
    block_rows = query_total // 4
    factor = head_dim ** (-0.5)

    def one_sample(operands):
        query_rows, key_sample, value_sample, usable_row = operands
        blocks = query_rows.reshape(4, block_rows, heads_device, head_dim)
        key_split = key_sample.reshape(key_sample.shape[0], heads_device, head_dim)
        value_split = value_sample.reshape(value_sample.shape[0], heads_device, head_dim)

        def one_block(block):
            return attend(block, key_split, value_split, usable_row, factor)

        outputs = lax.map(one_block, blocks)
        return outputs.reshape(query_total, heads_device * head_dim)

    head_output = lax.map(one_sample, (query_heads, key_heads, value_heads, usable))
    attention = lax.all_to_all(head_output, "seq", split_axis=1, concat_axis=2, tiled=True)
    text_attention = attention[:, :text_count]
    model_width = gate_table.shape[1]
    image_rows = attention[:, text_count:].reshape(samples * image_count, attention.shape[2])
    both_cores = lax.all_gather(image_rows, "tp", axis=0, tiled=True)
    half_columns = jnp.dot(
        both_cores,
        lax.all_gather(out_weight, "seq", axis=0, tiled=True),
        preferred_element_type=jnp.float32,
    )
    branch = lax.all_to_all(
        half_columns.astype(jnp.bfloat16), "tp", split_axis=0, concat_axis=1, tiled=True
    ).astype(half_columns.dtype)
    table_rows = gate_table.shape[0]
    selector = (strata[:, None] == jnp.arange(table_rows, dtype=jnp.int32)[None, :]).astype(
        jnp.bfloat16
    )
    gate_rows = jnp.dot(selector, gate_table, preferred_element_type=jnp.float32)
    combined = image_state.astype(jnp.float32) + gate_rows[:, None, :] * branch.reshape(
        samples, image_count, model_width
    )
    error_terms = combined - target.astype(jnp.float32)
    partial_sum = jnp.sum(error_terms * error_terms)
    total_sum = lax.psum(partial_sum, ("seq", "dp", "tp"))
    element_count = (
        samples * image_count * model_width * seq_count * core_count * lax.axis_size("dp")
    )
    flow_loss = (total_sum / element_count).reshape(1)
    return (combined.astype(jnp.bfloat16), text_attention, flow_loss)


def norm_block(values, gains):
    shaped = values.astype(jnp.float32)
    inverse = lax.rsqrt(jnp.mean(shaped * shaped, axis=-1, keepdims=True) + SMALL)
    return (shaped * inverse * gains).astype(jnp.bfloat16)


def place(rank, cores):
    return {"seq": rank // cores, "tp": rank % cores}


def attend_kernel(
    count, cores, factor,
    qt, qi, kt, ki, vt, vi, gains, bias,
    pair, text_out,
    qb, kb, vb, ob, send, recv, osend, orecv, fsend, frecv,
):
    text, image = qt.shape[1], qi.shape[1]
    rows = text + image
    wide = qb.shape[1]
    dim = gains.shape[1]
    heads = wide // dim
    core = lax.axis_index("tp")
    me = lax.axis_index("seq") * cores + core
    other = lax.rem(core + 1, cores)

    barrier = pltpu.get_barrier_semaphore()
    for o in range(1, count):
        pl.semaphore_signal(
            barrier, inc=1, device_id=place(lax.rem(me + o, count), cores), device_id_type=MESH
        )
    pl.semaphore_wait(barrier, count - 1)

    def block(buffer, rank, start, size):
        return buffer.at[pl.ds(pl.multiple_of(rank * rows + start, 16), size)]

    def columns(rank):
        return pl.ds(pl.multiple_of(rank * wide, wide), wide)

    tensors = ((kt, ki, kb), (vt, vi, vb), (qt, qi, qb))

    def inward(o, n):
        peer = lax.rem(me + o, count)
        out = []
        for part, (source, start, size) in enumerate(
            ((tensors[n][0], 0, text), (tensors[n][1], text, image))
        ):
            out.append((
                source.at[0, :, columns(peer)],
                block(tensors[n][2], me, start, size),
                send.at[o, 2 * n + part],
                recv.at[o, 2 * n + part],
                peer,
            ))
        return out

    def remote(args):
        src, dst, s, r, peer = args
        return pltpu.make_async_remote_copy(
            src_ref=src, dst_ref=dst, send_sem=s, recv_sem=r,
            device_id=place(peer, cores), device_id_type=MESH,
        )

    def near(args):
        src, dst, s, r, peer = args
        return pltpu.make_async_copy(src, dst, r)

    for n in range(3):
        for o in range(1, count):
            for a in inward(o, n):
                remote(a).start()
        for a in inward(0, n):
            near(a).start()

    row = lax.broadcasted_iota(jnp.int32, (rows, dim), 0)
    query_gain = jnp.where(row < text, gains[2:3, :], gains[0:1, :])
    key_gain = jnp.where(row < text, gains[3:4, :], gains[1:2, :])

    def take(buffer, rank, gain):
        at = pl.ds(pl.multiple_of(rank * rows, 16), rows)
        for h in range(heads):
            cols = slice(h * dim, (h + 1) * dim)
            buffer[at, cols] = norm_block(buffer[at, cols], gain)

    def outward(o):
        source = lax.rem(me - o + count, count)
        home = source % cores
        return [
            (block(ob, source, 0, text), text_out.at[0, :, columns(me)],
             osend.at[o, 0], orecv.at[o, 0], source),
            (block(ob, source, text, image),
             pair.at[pl.ds(pl.multiple_of(home * image, 16), image), columns(me)],
             osend.at[o, 1], orecv.at[o, 1], source),
        ]

    def work(o):
        source = lax.rem(me - o + count, count)
        take(qb, source, query_gain)
        at = pl.ds(pl.multiple_of(source * rows, 16), rows)
        for h in range(heads):
            cols = slice(h * dim, (h + 1) * dim)
            scores = lax.dot_general(
                qb[at, cols], kb[:, cols], (((1,), (1,)), ((), ())),
                preferred_element_type=jnp.float32,
            ) * factor + bias[...]
            powers = jnp.exp(scores - jnp.max(scores, axis=1, keepdims=True))
            scale = 1.0 / jnp.sum(powers, axis=1, keepdims=True)
            weights = (powers * scale).astype(jnp.bfloat16)
            ob[at, cols] = jnp.dot(
                weights, vb[:, cols], preferred_element_type=jnp.float32
            ).astype(jnp.bfloat16)

    def wait_recv(o, n):
        for a in inward(o, n):
            remote(a).wait_recv()

    for n in range(3):
        for a in inward(0, n):
            near(a).wait()
    take(kb, me, key_gain)

    def keys(o, carry):
        wait_recv(o, 0)
        take(kb, lax.rem(me - o + count, count), key_gain)
        return carry

    lax.fori_loop(1, count, keys, 0)

    def values(o, carry):
        wait_recv(o, 1)
        return carry

    lax.fori_loop(1, count, values, 0)

    work(0)
    for a in outward(0):
        near(a).start()

    def queries(o, carry):
        wait_recv(o, 2)
        work(o)
        for a in outward(o):
            remote(a).start()
        return carry

    lax.fori_loop(1, count, queries, 0)

    def share(o):
        sender = lax.rem(me + o, count)
        mine = pl.ds(pl.multiple_of(core * image, 16), image)
        return pltpu.make_async_remote_copy(
            src_ref=pair.at[mine, columns(sender)], dst_ref=pair.at[mine, columns(sender)],
            send_sem=fsend.at[o], recv_sem=frecv.at[o],
            device_id={"tp": other}, device_id_type=MESH,
        )

    for a in outward(0):
        near(a).wait()
    share(0).start()

    def homes(o, carry):
        for a in outward(o):
            remote(a).wait_recv()
        share(o).start()
        return carry

    lax.fori_loop(1, count, homes, 0)

    def ends(o, carry):
        share(o).wait()
        return carry

    lax.fori_loop(0, count, ends, 0)

    def drain(o, carry):
        for n in range(3):
            for a in inward(o, n):
                remote(a).wait_send()
        for a in outward(o):
            remote(a).wait_send()
        return carry

    lax.fori_loop(1, count, drain, 0)


def project_kernel(
    sizes, tile,
    pair, weight, state, target, gate,
    velocity, loss,
    acc, out, into, terms, send, recv, tsend, trecv,
):
    names = ("seq", "dp", "tp")
    image = state.shape[1]
    half = weight.shape[1]
    where = [lax.axis_index(n) for n in names]
    core = where[2]
    other = lax.rem(core + 1, sizes[2])
    total = sizes[0] * sizes[1] * sizes[2]
    me = (where[0] * sizes[1] + where[1]) * sizes[2] + core

    def device(rank):
        return {
            "seq": rank // (sizes[1] * sizes[2]),
            "dp": rank // sizes[2] % sizes[1],
            "tp": rank % sizes[2],
        }

    barrier = pltpu.get_barrier_semaphore()
    for o in range(1, total):
        pl.semaphore_signal(
            barrier, inc=1, device_id=device(lax.rem(me + o, total)), device_id_type=MESH
        )

    theirs = pl.ds(pl.multiple_of(other * image, 16), image)
    mine = pl.ds(pl.multiple_of(core * image, 16), image)
    tiles = half // tile

    def cross(j):
        cols = slice(j * tile, (j + 1) * tile)
        return pltpu.make_async_remote_copy(
            src_ref=out.at[:, cols], dst_ref=into.at[:, cols],
            send_sem=send.at[j], recv_sem=recv.at[j],
            device_id={"tp": other}, device_id_type=MESH,
        )

    for j in range(tiles):
        cols = slice(j * tile, (j + 1) * tile)
        acc[:, cols] = jnp.dot(
            pair[...], weight[:, cols], preferred_element_type=jnp.float32
        )
        out[:, cols] = acc[theirs, cols].astype(jnp.bfloat16)
        if j == 0:
            pl.semaphore_wait(barrier, total - 1)
        cross(j).start()

    def finish(branch, base, size):
        cols = pl.ds(pl.multiple_of(base, 128), size)
        combined = state[0, :, cols].astype(jnp.float32) + gate[:, cols] * branch
        velocity[0, :, cols] = combined.astype(jnp.bfloat16)
        error = combined - target[0, :, cols].astype(jnp.float32)
        squares = error * error
        lanes = squares[:, 0:128]
        for k in range(1, size // 128):
            lanes = lanes + squares[:, k * 128 : (k + 1) * 128]
        return jnp.sum(lanes, axis=0, keepdims=True)

    partial = jnp.zeros((1, 128), jnp.float32)
    for j in range(tiles):
        partial += finish(
            acc[mine, j * tile : (j + 1) * tile], core * half + j * tile, tile
        )
    for j in range(tiles):
        cross(j).wait_recv()
        partial += finish(
            into[:, j * tile : (j + 1) * tile].astype(jnp.float32), other * half + j * tile, tile
        )
    terms[0] = jnp.broadcast_to(partial, terms.shape[1:])

    def tell(o):
        return pltpu.make_async_remote_copy(
            src_ref=terms.at[0], dst_ref=terms.at[o],
            send_sem=tsend.at[o], recv_sem=trecv.at[o],
            device_id=device(lax.rem(me + o, total)), device_id_type=MESH,
        )

    for o in range(1, total):
        tell(o).start()
    for j in range(tiles):
        cross(j).wait_send()
    for o in range(1, total):
        tell(o).wait()
    loss[...] = jnp.sum(terms[...], axis=0)


def fast(
    query_image,
    key_image,
    value_image,
    query_text,
    key_text,
    value_text,
    image_query_gain,
    image_key_gain,
    text_query_gain,
    text_key_gain,
    text_length,
    strata,
    image_state,
    target,
    out_weight,
    gate_table,
):
    image = query_image.shape[1]
    text = query_text.shape[1]
    rows = image + text
    attn = query_image.shape[2]
    dim = image_query_gain.shape[0]
    width = gate_table.shape[1]
    seq, cores, dp, grp = (lax.axis_size(n) for n in ("seq", "tp", "dp", "grp"))
    count = seq * cores
    wide = attn // count
    copies = grp * dp
    piece = out_weight.shape[0] // copies
    copy_index = lax.axis_index("grp") * dp + lax.axis_index("dp")
    weight = lax.all_gather(
        lax.dynamic_slice_in_dim(out_weight, copy_index * piece, piece, 0),
        ("seq", "grp", "dp"), axis=0, tiled=True,
    )
    key_index = jnp.arange(count * rows, dtype=jnp.int32)
    within = key_index % rows
    usable = (within >= text) | (key_index // rows * text + within < text_length[0])
    bias = jnp.where(usable, 0.0, -1e30).astype(jnp.float32)[None, :]
    gains = jnp.stack([image_query_gain, image_key_gain, text_query_gain, text_key_gain])
    table_rows = gate_table.shape[0]
    selector = (strata[:, None] == jnp.arange(table_rows, dtype=jnp.int32)[None, :]).astype(
        jnp.bfloat16
    )
    gate = jnp.dot(selector, gate_table, preferred_element_type=jnp.float32)
    dma = pltpu.SemaphoreType.DMA
    bf16 = jnp.bfloat16
    pair, text_attention = pl.pallas_call(
        functools.partial(attend_kernel, count, cores, dim ** (-0.5)),
        out_shape=(
            jax.ShapeDtypeStruct((cores * image, attn), bf16),
            jax.ShapeDtypeStruct((1, text, attn), bf16),
        ),
        in_specs=[ANY] * 6 + [VMEM] * 2,
        out_specs=(VMEM, VMEM),
        scratch_shapes=[pltpu.VMEM((count * rows, wide), bf16)] * 4
        + [dma((count, 6)), dma((count, 6)), dma((count, 2)), dma((count, 2)), dma((count,)), dma((count,))],
        compiler_params=pltpu.CompilerParams(
            collective_id=0, has_side_effects=True, vmem_limit_bytes=24 * 2**20
        ),
        cost_estimate=pl.CostEstimate(
            flops=4 * count * rows * count * rows * wide,
            bytes_accessed=200_000_000,
            transcendentals=count * rows * count * rows,
        ),
    )(query_text, query_image, key_text, key_image, value_text, value_image, gains, bias)
    half = width // cores
    tile = half // 3 if half % 384 == 0 else half
    sizes = (seq, dp, cores)
    total = seq * dp * cores
    velocity, loss = pl.pallas_call(
        functools.partial(project_kernel, sizes, tile),
        out_shape=(
            jax.ShapeDtypeStruct((1, image, width), bf16),
            jax.ShapeDtypeStruct((8, 128), jnp.float32),
        ),
        in_specs=[VMEM] * 5,
        out_specs=(VMEM, VMEM),
        scratch_shapes=[
            pltpu.VMEM((cores * image, half), jnp.float32),
            pltpu.VMEM((image, half), bf16),
            pltpu.VMEM((image, half), bf16),
            pltpu.VMEM((total, 8, 128), jnp.float32),
            dma((half // tile,)), dma((half // tile,)), dma((total,)), dma((total,)),
        ],
        compiler_params=pltpu.CompilerParams(
            collective_id=1, has_side_effects=True, vmem_limit_bytes=40 * 2**20
        ),
    )(pair, weight, image_state, target, gate)
    flow_loss = (jnp.sum(loss[0]) / (image * width * total)).reshape(1)
    return velocity, text_attention, flow_loss


def solution(mesh):
    def body(*operands):
        samples, image, attn = operands[0].shape
        heads = attn // operands[6].shape[0]
        shape = dict(mesh.shape)
        fits = (
            samples == 1
            and shape["tp"] == 2
            and heads % (shape["seq"] * shape["tp"]) == 0
            and operands[14].shape[0] % (16 * shape["grp"] * shape["dp"]) == 0
        )
        return fast(*operands) if fits else local(*operands)

    placed = (
        P(("grp", "dp"), ("seq", "tp"), None),
        P(("grp", "dp"), ("seq", "tp"), None),
        P(("grp", "dp"), ("seq", "tp"), None),
        P(("grp", "dp"), ("seq", "tp"), None),
        P(("grp", "dp"), ("seq", "tp"), None),
        P(("grp", "dp"), ("seq", "tp"), None),
        P(),
        P(),
        P(),
        P(),
        P(("grp", "dp")),
        P(("grp", "dp")),
        P(("grp", "dp"), ("seq", "tp"), None),
        P(("grp", "dp"), ("seq", "tp"), None),
        P("seq", "tp"),
        P(),
    )
    return jax.shard_map(
        body,
        mesh=mesh,
        in_specs=placed,
        out_specs=(
            P(("grp", "dp"), ("seq", "tp"), None),
            P(("grp", "dp"), ("seq", "tp"), None),
            P("grp"),
        ),
        check_vma=False,
    )
```

```python
import functools

import jax
import jax.numpy as jnp
import numpy as np
from jax import lax
from jax.experimental import pallas as pl
from jax.experimental.pallas import tpu as pltpu
from jax.sharding import PartitionSpec as P

MESH = pl.DeviceIdType.MESH
VMEM = pl.BlockSpec(memory_space=pltpu.VMEM)
ANY = pl.BlockSpec(memory_space=pl.ANY)
SMALL = 1e-06


def head_norm(values, gain_vector):
    head_dim = gain_vector.shape[0]
    columns = values.shape[-1]
    shaped = values.astype(jnp.float32).reshape(values.shape[:-1] + (columns // head_dim, head_dim))
    inverse = lax.rsqrt(jnp.mean(shaped * shaped, axis=-1, keepdims=True) + 1e-06)
    return (shaped * inverse * gain_vector).reshape(values.shape).astype(jnp.bfloat16)


def attend(query_block, key_split, value_split, usable, factor):
    scores = (
        jnp.einsum("qhd,khd->hqk", query_block, key_split, preferred_element_type=jnp.float32)
        * factor
    )
    scores = jnp.where(usable[None, None, :], scores, -1e30)
    row_max = jnp.max(scores, axis=2, keepdims=True)
    powers = jnp.exp(scores - row_max)
    weights = (powers / jnp.sum(powers, axis=2, keepdims=True)).astype(jnp.bfloat16)
    return jnp.einsum(
        "hqk,khd->qhd", weights, value_split, preferred_element_type=jnp.float32
    ).astype(jnp.bfloat16)


def local(
    query_image,
    key_image,
    value_image,
    query_text,
    key_text,
    value_text,
    image_query_gain,
    image_key_gain,
    text_query_gain,
    text_key_gain,
    text_length,
    strata,
    image_state,
    target,
    out_weight,
    gate_table,
):
    samples = query_image.shape[0]
    image_count = query_image.shape[1]
    text_count = query_text.shape[1]
    local_rows = image_count + text_count
    head_dim = image_query_gain.shape[0]
    seq_count = lax.axis_size("seq")
    core_count = lax.axis_size("tp")
    queries = jnp.concatenate(
        [head_norm(query_text, text_query_gain), head_norm(query_image, image_query_gain)], axis=1
    )
    keys_local = jnp.concatenate(
        [head_norm(key_text, text_key_gain), head_norm(key_image, image_key_gain)], axis=1
    )
    values_local = jnp.concatenate([value_text, value_image], axis=1)
    key_index = jnp.arange(seq_count * core_count * local_rows, dtype=jnp.int32)
    within = key_index % local_rows
    query_heads, key_rows, value_rows = (
        lax.all_to_all(queries, "seq", split_axis=2, concat_axis=1, tiled=True),
        lax.all_to_all(keys_local, "seq", split_axis=2, concat_axis=1, tiled=True),
        lax.all_to_all(values_local, "seq", split_axis=2, concat_axis=1, tiled=True),
    )
    key_heads, value_heads = (
        lax.all_gather(key_rows, "tp", axis=1, tiled=True),
        lax.all_gather(value_rows, "tp", axis=1, tiled=True),
    )
    core_shard = key_index // (seq_count * local_rows)
    seq_shard = key_index // local_rows % seq_count
    text_place = (seq_shard * core_count + core_shard) * text_count + within
    usable = (within[None, :] >= text_count) | (text_place[None, :] < text_length[:, None])
    query_total = query_heads.shape[1]
    heads_device = query_heads.shape[2] // head_dim
    block_rows = query_total // 4
    factor = head_dim ** (-0.5)

    def one_sample(operands):
        query_rows, key_sample, value_sample, usable_row = operands
        blocks = query_rows.reshape(4, block_rows, heads_device, head_dim)
        key_split = key_sample.reshape(key_sample.shape[0], heads_device, head_dim)
        value_split = value_sample.reshape(value_sample.shape[0], heads_device, head_dim)

        def one_block(block):
            return attend(block, key_split, value_split, usable_row, factor)

        outputs = lax.map(one_block, blocks)
        return outputs.reshape(query_total, heads_device * head_dim)

    head_output = lax.map(one_sample, (query_heads, key_heads, value_heads, usable))
    attention = lax.all_to_all(head_output, "seq", split_axis=1, concat_axis=2, tiled=True)
    text_attention = attention[:, :text_count]
    model_width = gate_table.shape[1]
    image_rows = attention[:, text_count:].reshape(samples * image_count, attention.shape[2])
    both_cores = lax.all_gather(image_rows, "tp", axis=0, tiled=True)
    half_columns = jnp.dot(
        both_cores,
        lax.all_gather(out_weight, "seq", axis=0, tiled=True),
        preferred_element_type=jnp.float32,
    )
    branch = lax.all_to_all(
        half_columns.astype(jnp.bfloat16), "tp", split_axis=0, concat_axis=1, tiled=True
    ).astype(half_columns.dtype)
    table_rows = gate_table.shape[0]
    selector = (strata[:, None] == jnp.arange(table_rows, dtype=jnp.int32)[None, :]).astype(
        jnp.bfloat16
    )
    gate_rows = jnp.dot(selector, gate_table, preferred_element_type=jnp.float32)
    combined = image_state.astype(jnp.float32) + gate_rows[:, None, :] * branch.reshape(
        samples, image_count, model_width
    )
    error_terms = combined - target.astype(jnp.float32)
    partial_sum = jnp.sum(error_terms * error_terms)
    total_sum = lax.psum(partial_sum, ("seq", "dp", "tp"))
    element_count = (
        samples * image_count * model_width * seq_count * core_count * lax.axis_size("dp")
    )
    flow_loss = (total_sum / element_count).reshape(1)
    return (combined.astype(jnp.bfloat16), text_attention, flow_loss)


def norm_block(values, gains):
    shaped = values.astype(jnp.float32)
    inverse = lax.rsqrt(jnp.mean(shaped * shaped, axis=-1, keepdims=True) + SMALL)
    return (shaped * inverse * gains).astype(jnp.bfloat16)


def whole_kernel(
    sizes, factor, tile,
    qt, qi, kt, ki, vt, vi,
    weight, state_in, target_in, table_in,
    gain_qi, gain_ki, gain_qt, gain_kt, key_place, length, stratum,
    velocity, text_out, loss,
    qb, kb, vb, ob, pair, wb, state, target, table,
    acc, out, into, terms,
    send, recv, osend, orecv, fsend, frecv,
    wsend, wrecv, xsend, xrecv, dsend, drecv,
    lsem, psend, precv, tsend, trecv,
):
    seq, dp, cores = sizes
    count = seq * cores
    total = seq * dp * cores
    text, image = qt.shape[1], qi.shape[1]
    rows = text + image
    wide = qb.shape[1]
    dim = gain_qi.shape[1]
    heads = wide // dim
    half = weight.shape[1]
    z = lax.axis_index("seq")
    x = lax.axis_index("dp")
    y = lax.axis_index("grp")
    core = lax.axis_index("tp")
    me = z * cores + core
    other = lax.rem(core + 1, cores)
    group = (z * dp + x) * cores + core

    def place(rank):
        return {"seq": rank // cores, "tp": rank % cores}

    def member(rank):
        return {
            "seq": rank // (dp * cores),
            "dp": rank // cores % dp,
            "tp": rank % cores,
        }

    beside = ({"dp": 1 - x}, {"grp": 1 - y})

    barrier = pltpu.get_barrier_semaphore()
    for o in range(1, total):
        pl.semaphore_signal(
            barrier, inc=1, device_id=member(lax.rem(group + o, total)), device_id_type=MESH
        )
    pl.semaphore_signal(barrier, inc=1, device_id=beside[1], device_id_type=MESH)

    local_copies = [
        pltpu.make_async_copy(
            weight, wb.at[pl.ds(pl.multiple_of(z * weight.shape[0], 16), weight.shape[0])], lsem.at[0]
        ),
        pltpu.make_async_copy(state_in, state, lsem.at[1]),
        pltpu.make_async_copy(target_in, target, lsem.at[2]),
        pltpu.make_async_copy(table_in, table, lsem.at[3]),
    ]

    def remote(src, dst, s, r, device):
        return pltpu.make_async_remote_copy(
            src_ref=src, dst_ref=dst, send_sem=s, recv_sem=r,
            device_id=device, device_id_type=MESH,
        )

    depth = weight.shape[0]
    piece = depth // 4
    quarter = y * 2 + x

    def spot(block, q, start, size):
        return wb.at[pl.ds(pl.multiple_of(block * depth + q * piece + start, 16), size)]

    def hop(way, k):
        step = 1 - 2 * way
        origin = z - step * (k - 1)
        source = (
            weight.at[pl.ds(pl.multiple_of(quarter * piece, 16), piece)]
            if k == 1 else spot(origin, quarter, 0, piece)
        )
        return remote(
            source, spot(origin, quarter, 0, piece), wsend.at[way, k], wrecv.at[way, k],
            {"seq": z + step},
        )

    def landed(way, k):
        step = 1 - 2 * way
        origin = z - step * k
        ref = spot(origin, quarter, 0, piece)
        return remote(ref, ref, wsend.at[way, k], wrecv.at[way, k], {"seq": z - step})

    def has(way, k):
        return z >= k if way == 0 else z < seq - k

    def sends(way, k):
        onward = z < seq - 1 if way == 0 else z > 0
        return onward if k == 1 else jnp.logical_and(onward, has(way, k - 1))

    def side(axis, way, k):
        origin = z - (1 - 2 * way) * k
        ref = spot(origin, quarter, 0, piece)
        return remote(ref, ref, xsend.at[axis, way, k], xrecv.at[axis, way, k], beside[axis])

    def side_quarter(axis):
        return y * 2 + (1 - x) if axis == 0 else (1 - y) * 2 + x

    def side_landed(axis, way, k):
        origin = z - (1 - 2 * way) * k
        ref = spot(origin, side_quarter(axis), 0, piece)
        return remote(ref, ref, xsend.at[axis, way, k], xrecv.at[axis, way, k], beside[axis])

    def corner(axis, way, k):
        origin = z - (1 - 2 * way) * k
        ref = spot(origin, side_quarter(axis), axis * (piece // 2), piece // 2)
        return remote(
            ref, ref, dsend.at[axis, way, k], drecv.at[axis, way, k], beside[1 - axis]
        )

    def corner_landed(axis, way, k):
        origin = z - (1 - 2 * way) * k
        ref = spot(origin, (1 - y) * 2 + (1 - x), axis * (piece // 2), piece // 2)
        return remote(
            ref, ref, dsend.at[axis, way, k], drecv.at[axis, way, k], beside[1 - axis]
        )

    def spread(k):
        for way in range(2):
            @pl.when(has(way, k))
            def _():
                landed(way, k).wait_recv()
                if k + 1 < seq:
                    @pl.when(sends(way, k + 1))
                    def _():
                        hop(way, k + 1).start()
                side(0, way, k).start()
                side(1, way, k).start()

    def corners(k):
        for way in range(2):
            @pl.when(has(way, k))
            def _():
                for axis in range(2):
                    side_landed(axis, way, k).wait_recv()
                    corner(axis, way, k).start()

    def settle(k):
        for way in range(2):
            @pl.when(sends(way, k))
            def _():
                hop(way, k).wait_send()

            @pl.when(has(way, k))
            def _():
                for axis in range(2):
                    side(axis, way, k).wait_send()
                    corner(axis, way, k).wait_send()
                    corner_landed(axis, way, k).wait_recv()

    def block(buffer, rank, start, size):
        return buffer.at[pl.ds(pl.multiple_of(rank * rows + start, 16), size)]

    def columns(rank):
        return pl.ds(pl.multiple_of(rank * wide, wide), wide)

    tensors = ((kt, ki, kb), (vt, vi, vb), (qt, qi, qb))

    def inward(o, n):
        peer = lax.rem(me + o, count)
        out = []
        for part, (source, start, size) in enumerate(
            ((tensors[n][0], 0, text), (tensors[n][1], text, image))
        ):
            out.append((
                source.at[0, :, columns(peer)],
                block(tensors[n][2], me, start, size),
                send.at[o, 2 * n + part],
                recv.at[o, 2 * n + part],
                place(peer),
            ))
        return out

    def near(args):
        return pltpu.make_async_copy(args[0], args[1], args[3])

    def scatter(n):
        for o in range(1, count):
            for a in inward(o, n):
                remote(*a).start()

    row = lax.broadcasted_iota(jnp.int32, (rows, dim), 0)

    def take(buffer, rank, text_gain, image_gain):
        gain = jnp.where(row < text, text_gain[...], image_gain[...])
        at = pl.ds(pl.multiple_of(rank * rows, 16), rows)
        for h in range(heads):
            cols = slice(h * dim, (h + 1) * dim)
            buffer[at, cols] = norm_block(buffer[at, cols], gain)

    def outward(o):
        source = lax.rem(me - o + count, count)
        home = source % cores
        return [
            (block(ob, source, 0, text), text_out.at[0, :, columns(me)],
             osend.at[o, 0], orecv.at[o, 0], place(source)),
            (block(ob, source, text, image),
             pair.at[pl.ds(pl.multiple_of(home * image, 16), image), columns(me)],
             osend.at[o, 1], orecv.at[o, 1], place(source)),
        ]

    bias = jnp.where(key_place[...] < length[0], 0.0, -1e30).astype(jnp.float32)

    def work(o):
        source = lax.rem(me - o + count, count)
        take(qb, source, gain_qt, gain_qi)
        at = pl.ds(pl.multiple_of(source * rows, 16), rows)
        for h in range(heads):
            cols = slice(h * dim, (h + 1) * dim)
            scores = lax.dot_general(
                qb[at, cols], kb[:, cols], (((1,), (1,)), ((), ())),
                preferred_element_type=jnp.float32,
            ) * factor + bias
            powers = jnp.exp(scores - jnp.max(scores, axis=1, keepdims=True))
            scale = 1.0 / jnp.sum(powers, axis=1, keepdims=True)
            weights = (powers * scale).astype(jnp.bfloat16)
            ob[at, cols] = jnp.dot(
                weights, vb[:, cols], preferred_element_type=jnp.float32
            ).astype(jnp.bfloat16)

    def wait_recv(o, n):
        for a in inward(o, n):
            remote(*a).wait_recv()

    for n in range(3):
        for a in inward(0, n):
            near(a).start()
    pl.semaphore_wait(barrier, total)
    for way in range(2):
        @pl.when(sends(way, 1))
        def _():
            hop(way, 1).start()
    scatter(0)
    for c in local_copies:
        c.start()
    for n in range(3):
        for a in inward(0, n):
            near(a).wait()
    take(kb, me, gain_kt, gain_ki)
    spread(1)
    scatter(1)

    def keys(o, carry):
        wait_recv(o, 0)
        take(kb, lax.rem(me - o + count, count), gain_kt, gain_ki)
        return carry

    if seq > 2:
        spread(2)
    scatter(2)
    lax.fori_loop(1, count, keys, 0)
    for k in range(3, seq):
        spread(k)
    corners(1)

    def values(o, carry):
        wait_recv(o, 1)
        return carry

    lax.fori_loop(1, count, values, 0)

    work(0)
    for a in outward(0):
        near(a).start()
    for k in range(2, seq - 1):
        corners(k)

    def queries(o, carry):
        wait_recv(o, 2)
        work(o)
        for a in outward(o):
            remote(*a).start()
        return carry

    lax.fori_loop(1, count, queries, 0)
    if seq > 2:
        corners(seq - 1)

    mine = pl.ds(pl.multiple_of(core * image, 16), image)
    theirs = pl.ds(pl.multiple_of(other * image, 16), image)

    def share(o):
        ref = pair.at[mine, columns(lax.rem(me + o, count))]
        return remote(ref, ref, fsend.at[o], frecv.at[o], {"tp": other})

    def shared(o):
        ref = pair.at[theirs, columns(lax.rem(z * cores + other + o, count))]
        return remote(ref, ref, fsend.at[o], frecv.at[o], {"tp": other})

    for a in outward(0):
        near(a).wait()
    share(0).start()
    for c in local_copies:
        c.wait()
    table_rows = table.shape[0]
    selector = lax.broadcasted_iota(jnp.int32, (16, table_rows), 1) == stratum[0]

    def homes(o, carry):
        for a in outward(o):
            src = a[0]
            where = lax.rem(me + o, count)
            dst = (
                text_out.at[0, :, columns(where)]
                if src.shape[0] == text
                else pair.at[mine, columns(where)]
            )
            remote(dst, dst, a[2], a[3], a[4]).wait_recv()
        share(o).start()
        return carry

    lax.fori_loop(1, count, homes, 0)

    def ends(o, carry):
        share(o).wait_send()
        shared(o).wait_recv()
        return carry

    lax.fori_loop(0, count, ends, 0)
    for k in range(1, seq):
        settle(k)

    tiles = half // tile

    def cross(j):
        cols = slice(j * tile, (j + 1) * tile)
        return remote(
            out.at[:, cols], into.at[:, cols], psend.at[j], precv.at[j], {"tp": other}
        )

    for j in range(tiles):
        cols = slice(j * tile, (j + 1) * tile)
        acc[:, cols] = jnp.dot(pair[...], wb[:, cols], preferred_element_type=jnp.float32)
        out[:, cols] = acc[theirs, cols].astype(jnp.bfloat16)
        cross(j).start()

    def finish(branch, base, size):
        cols = pl.ds(pl.multiple_of(base, 128), size)
        gate = jnp.dot(
            selector.astype(jnp.bfloat16), table[:, cols], preferred_element_type=jnp.float32
        )[0:1]
        combined = state[0, :, cols].astype(jnp.float32) + gate * branch
        velocity[0, :, cols] = combined.astype(jnp.bfloat16)
        error = combined - target[0, :, cols].astype(jnp.float32)
        squares = error * error
        lanes = squares[:, 0:128]
        for k in range(1, size // 128):
            lanes = lanes + squares[:, k * 128 : (k + 1) * 128]
        return jnp.sum(lanes, axis=0, keepdims=True)

    partial = jnp.zeros((1, 128), jnp.float32)
    for j in range(tiles):
        partial += finish(
            acc[mine, j * tile : (j + 1) * tile], core * half + j * tile, tile
        )
    for j in range(tiles):
        cross(j).wait_recv()
        partial += finish(
            into[:, j * tile : (j + 1) * tile].astype(jnp.float32), other * half + j * tile, tile
        )
    terms[0] = jnp.broadcast_to(partial, terms.shape[1:])

    def tell(o):
        return remote(
            terms.at[0], terms.at[o], tsend.at[o], trecv.at[o],
            member(lax.rem(group + o, total)),
        )

    for o in range(1, total):
        tell(o).start()
    for j in range(tiles):
        cross(j).wait_send()

    def drain(o, carry):
        for n in range(3):
            for a in inward(o, n):
                remote(*a).wait_send()
        for a in outward(o):
            remote(*a).wait_send()
        return carry

    lax.fori_loop(1, count, drain, 0)
    for o in range(1, total):
        tell(o).wait()
    whole = jnp.sum(jnp.sum(terms[...], axis=0)[0:1])
    loss[0] = whole / (image * velocity.shape[2] * total)


def fast(
    query_image,
    key_image,
    value_image,
    query_text,
    key_text,
    value_text,
    image_query_gain,
    image_key_gain,
    text_query_gain,
    text_key_gain,
    text_length,
    strata,
    image_state,
    target,
    out_weight,
    gate_table,
):
    image = query_image.shape[1]
    text = query_text.shape[1]
    rows = image + text
    attn = query_image.shape[2]
    dim = image_query_gain.shape[0]
    width = gate_table.shape[1]
    seq, cores, dp = (lax.axis_size(n) for n in ("seq", "tp", "dp"))
    sizes = (seq, dp, cores)
    count = seq * cores
    total = seq * dp * cores
    wide = attn // count
    half = width // cores
    tile = half // 3 if half % 384 == 0 else half
    key_index = np.arange(count * rows, dtype=np.int32)
    within = key_index % rows
    key_place = np.where(within < text, key_index // rows * text + within, -1)[None, :]
    dma = pltpu.SemaphoreType.DMA
    bf16 = jnp.bfloat16
    smem = pl.BlockSpec(memory_space=pltpu.SMEM)
    return pl.pallas_call(
        functools.partial(whole_kernel, sizes, dim ** (-0.5), tile),
        out_shape=(
            jax.ShapeDtypeStruct((1, image, width), bf16),
            jax.ShapeDtypeStruct((1, text, attn), bf16),
            jax.ShapeDtypeStruct((1,), jnp.float32),
        ),
        in_specs=[ANY] * 10 + [VMEM] * 5 + [smem] * 2,
        out_specs=(VMEM, VMEM, smem),
        scratch_shapes=[pltpu.VMEM((count * rows, wide), bf16)] * 4
        + [
            pltpu.VMEM((cores * image, attn), bf16),
            pltpu.VMEM((attn, half), bf16),
            pltpu.VMEM((1, image, width), bf16),
            pltpu.VMEM((1, image, width), bf16),
            pltpu.VMEM(gate_table.shape, bf16),
            pltpu.VMEM((cores * image, half), jnp.float32),
            pltpu.VMEM((image, half), bf16),
            pltpu.VMEM((image, half), bf16),
            pltpu.VMEM((total, 8, 128), jnp.float32),
            dma((count, 6)), dma((count, 6)), dma((count, 2)), dma((count, 2)),
            dma((count,)), dma((count,)),
            dma((2, seq)), dma((2, seq)), dma((2, 2, seq)), dma((2, 2, seq)),
            dma((2, 2, seq)), dma((2, 2, seq)),
            dma((4,)), dma((half // tile,)), dma((half // tile,)), dma((total,)), dma((total,)),
        ],
        compiler_params=pltpu.CompilerParams(
            collective_id=0, has_side_effects=True, vmem_limit_bytes=60 * 2**20
        ),
    )(
        query_text, query_image, key_text, key_image, value_text, value_image,
        out_weight, image_state, target, gate_table,
        image_query_gain[None], image_key_gain[None], text_query_gain[None], text_key_gain[None],
        jnp.asarray(key_place, jnp.int32), text_length, strata,
    )


def solution(mesh):
    def body(*operands):
        samples, image, attn = operands[0].shape
        heads = attn // operands[6].shape[0]
        shape = dict(mesh.shape)
        fits = (
            samples == 1
            and shape["tp"] == 2
            and heads % (shape["seq"] * shape["tp"]) == 0
            and shape["grp"] == 2
            and shape["dp"] == 2
            and operands[14].shape[0] % 128 == 0
        )
        return fast(*operands) if fits else local(*operands)

    placed = (
        P(("grp", "dp"), ("seq", "tp"), None),
        P(("grp", "dp"), ("seq", "tp"), None),
        P(("grp", "dp"), ("seq", "tp"), None),
        P(("grp", "dp"), ("seq", "tp"), None),
        P(("grp", "dp"), ("seq", "tp"), None),
        P(("grp", "dp"), ("seq", "tp"), None),
        P(),
        P(),
        P(),
        P(),
        P(("grp", "dp")),
        P(("grp", "dp")),
        P(("grp", "dp"), ("seq", "tp"), None),
        P(("grp", "dp"), ("seq", "tp"), None),
        P("seq", "tp"),
        P(),
    )
    return jax.shard_map(
        body,
        mesh=mesh,
        in_specs=placed,
        out_specs=(
            P(("grp", "dp"), ("seq", "tp"), None),
            P(("grp", "dp"), ("seq", "tp"), None),
            P("grp"),
        ),
        check_vma=False,
    )
```

```python
import functools

import jax
import jax.numpy as jnp
import numpy as np
from jax import lax
from jax.experimental import pallas as pl
from jax.experimental.pallas import tpu as pltpu
from jax.sharding import PartitionSpec as P

MESH = pl.DeviceIdType.MESH
VMEM = pl.BlockSpec(memory_space=pltpu.VMEM)
ANY = pl.BlockSpec(memory_space=pl.ANY)
SMALL = 1e-06


def head_norm(values, gain_vector):
    head_dim = gain_vector.shape[0]
    columns = values.shape[-1]
    shaped = values.astype(jnp.float32).reshape(values.shape[:-1] + (columns // head_dim, head_dim))
    inverse = lax.rsqrt(jnp.mean(shaped * shaped, axis=-1, keepdims=True) + 1e-06)
    return (shaped * inverse * gain_vector).reshape(values.shape).astype(jnp.bfloat16)


def attend(query_block, key_split, value_split, usable, factor):
    scores = (
        jnp.einsum("qhd,khd->hqk", query_block, key_split, preferred_element_type=jnp.float32)
        * factor
    )
    scores = jnp.where(usable[None, None, :], scores, -1e30)
    row_max = jnp.max(scores, axis=2, keepdims=True)
    powers = jnp.exp(scores - row_max)
    weights = (powers / jnp.sum(powers, axis=2, keepdims=True)).astype(jnp.bfloat16)
    return jnp.einsum(
        "hqk,khd->qhd", weights, value_split, preferred_element_type=jnp.float32
    ).astype(jnp.bfloat16)


def local(
    query_image,
    key_image,
    value_image,
    query_text,
    key_text,
    value_text,
    image_query_gain,
    image_key_gain,
    text_query_gain,
    text_key_gain,
    text_length,
    strata,
    image_state,
    target,
    out_weight,
    gate_table,
):
    samples = query_image.shape[0]
    image_count = query_image.shape[1]
    text_count = query_text.shape[1]
    local_rows = image_count + text_count
    head_dim = image_query_gain.shape[0]
    seq_count = lax.axis_size("seq")
    core_count = lax.axis_size("tp")
    queries = jnp.concatenate(
        [head_norm(query_text, text_query_gain), head_norm(query_image, image_query_gain)], axis=1
    )
    keys_local = jnp.concatenate(
        [head_norm(key_text, text_key_gain), head_norm(key_image, image_key_gain)], axis=1
    )
    values_local = jnp.concatenate([value_text, value_image], axis=1)
    key_index = jnp.arange(seq_count * core_count * local_rows, dtype=jnp.int32)
    within = key_index % local_rows
    query_heads, key_rows, value_rows = (
        lax.all_to_all(queries, "seq", split_axis=2, concat_axis=1, tiled=True),
        lax.all_to_all(keys_local, "seq", split_axis=2, concat_axis=1, tiled=True),
        lax.all_to_all(values_local, "seq", split_axis=2, concat_axis=1, tiled=True),
    )
    key_heads, value_heads = (
        lax.all_gather(key_rows, "tp", axis=1, tiled=True),
        lax.all_gather(value_rows, "tp", axis=1, tiled=True),
    )
    core_shard = key_index // (seq_count * local_rows)
    seq_shard = key_index // local_rows % seq_count
    text_place = (seq_shard * core_count + core_shard) * text_count + within
    usable = (within[None, :] >= text_count) | (text_place[None, :] < text_length[:, None])
    query_total = query_heads.shape[1]
    heads_device = query_heads.shape[2] // head_dim
    block_rows = query_total // 4
    factor = head_dim ** (-0.5)

    def one_sample(operands):
        query_rows, key_sample, value_sample, usable_row = operands
        blocks = query_rows.reshape(4, block_rows, heads_device, head_dim)
        key_split = key_sample.reshape(key_sample.shape[0], heads_device, head_dim)
        value_split = value_sample.reshape(value_sample.shape[0], heads_device, head_dim)

        def one_block(block):
            return attend(block, key_split, value_split, usable_row, factor)

        outputs = lax.map(one_block, blocks)
        return outputs.reshape(query_total, heads_device * head_dim)

    head_output = lax.map(one_sample, (query_heads, key_heads, value_heads, usable))
    attention = lax.all_to_all(head_output, "seq", split_axis=1, concat_axis=2, tiled=True)
    text_attention = attention[:, :text_count]
    model_width = gate_table.shape[1]
    image_rows = attention[:, text_count:].reshape(samples * image_count, attention.shape[2])
    both_cores = lax.all_gather(image_rows, "tp", axis=0, tiled=True)
    half_columns = jnp.dot(
        both_cores,
        lax.all_gather(out_weight, "seq", axis=0, tiled=True),
        preferred_element_type=jnp.float32,
    )
    branch = lax.all_to_all(
        half_columns.astype(jnp.bfloat16), "tp", split_axis=0, concat_axis=1, tiled=True
    ).astype(half_columns.dtype)
    table_rows = gate_table.shape[0]
    selector = (strata[:, None] == jnp.arange(table_rows, dtype=jnp.int32)[None, :]).astype(
        jnp.bfloat16
    )
    gate_rows = jnp.dot(selector, gate_table, preferred_element_type=jnp.float32)
    combined = image_state.astype(jnp.float32) + gate_rows[:, None, :] * branch.reshape(
        samples, image_count, model_width
    )
    error_terms = combined - target.astype(jnp.float32)
    partial_sum = jnp.sum(error_terms * error_terms)
    total_sum = lax.psum(partial_sum, ("seq", "dp", "tp"))
    element_count = (
        samples * image_count * model_width * seq_count * core_count * lax.axis_size("dp")
    )
    flow_loss = (total_sum / element_count).reshape(1)
    return (combined.astype(jnp.bfloat16), text_attention, flow_loss)


def norm_block(values, gains):
    shaped = values.astype(jnp.float32)
    inverse = lax.rsqrt(jnp.mean(shaped * shaped, axis=-1, keepdims=True) + SMALL)
    return (shaped * inverse * gains).astype(jnp.bfloat16)


def whole_kernel(
    sizes, factor, tile,
    qt, qi, kt, ki, vt, vi,
    weight, state_in, target_in, table_in,
    gain_qi, gain_ki, gain_qt, gain_kt, key_place, length, stratum,
    velocity_out, text_out, loss,
    velocity, qb, kb, vb, ob, pair, wb, state, target, table,
    acc, out, into, terms,
    send, recv, osend, orecv, fsend, frecv,
    wsend, wrecv, xsend, xrecv, dsend, drecv,
    lsem, psend, precv, tsend, trecv,
):
    seq, dp, cores = sizes
    count = seq * cores
    total = seq * dp * cores
    text, image = qt.shape[1], qi.shape[1]
    rows = text + image
    wide = qb.shape[1]
    dim = gain_qi.shape[1]
    heads = wide // dim
    half = weight.shape[1]
    z = lax.axis_index("seq")
    x = lax.axis_index("dp")
    y = lax.axis_index("grp")
    core = lax.axis_index("tp")
    me = z * cores + core
    other = lax.rem(core + 1, cores)
    group = (z * dp + x) * cores + core

    def ahead(o):
        return lax.rem(z + o // cores, seq) * cores + lax.rem(core + o % cores, cores)

    def behind(o):
        return (
            lax.rem(z - o // cores + seq, seq) * cores
            + lax.rem(core - o % cores + cores, cores)
        )

    def turn(i):
        return i

    def place(rank):
        return {"seq": rank // cores, "tp": rank % cores}

    def member(rank):
        return {
            "seq": rank // (dp * cores),
            "dp": rank // cores % dp,
            "tp": rank % cores,
        }

    beside = ({"dp": 1 - x}, {"grp": 1 - y})

    barrier = pltpu.get_barrier_semaphore()
    for o in range(1, total):
        pl.semaphore_signal(
            barrier, inc=1, device_id=member(lax.rem(group + o, total)), device_id_type=MESH
        )
    pl.semaphore_signal(barrier, inc=1, device_id=beside[1], device_id_type=MESH)

    local_copies = [
        pltpu.make_async_copy(
            weight, wb.at[pl.ds(pl.multiple_of(z * weight.shape[0], 16), weight.shape[0])], lsem.at[0]
        ),
        pltpu.make_async_copy(state_in, state, lsem.at[1]),
        pltpu.make_async_copy(target_in, target, lsem.at[2]),
        pltpu.make_async_copy(table_in, table, lsem.at[3]),
    ]

    def remote(src, dst, s, r, device):
        return pltpu.make_async_remote_copy(
            src_ref=src, dst_ref=dst, send_sem=s, recv_sem=r,
            device_id=device, device_id_type=MESH,
        )

    depth = weight.shape[0]
    piece = depth // 4
    quarter = y * 2 + x

    def spot(block, q, start, size):
        return wb.at[pl.ds(pl.multiple_of(block * depth + q * piece + start, 16), size)]

    def hop(way, k):
        step = 1 - 2 * way
        origin = z - step * (k - 1)
        source = (
            weight.at[pl.ds(pl.multiple_of(quarter * piece, 16), piece)]
            if k == 1 else spot(origin, quarter, 0, piece)
        )
        return remote(
            source, spot(origin, quarter, 0, piece), wsend.at[way, k], wrecv.at[way, k],
            {"seq": z + step},
        )

    def landed(way, k):
        step = 1 - 2 * way
        origin = z - step * k
        ref = spot(origin, quarter, 0, piece)
        return remote(ref, ref, wsend.at[way, k], wrecv.at[way, k], {"seq": z - step})

    def has(way, k):
        return z >= k if way == 0 else z < seq - k

    def sends(way, k):
        onward = z < seq - 1 if way == 0 else z > 0
        return onward if k == 1 else jnp.logical_and(onward, has(way, k - 1))

    def side(axis, way, k):
        origin = z - (1 - 2 * way) * k
        ref = spot(origin, quarter, 0, piece)
        return remote(ref, ref, xsend.at[axis, way, k], xrecv.at[axis, way, k], beside[axis])

    def side_quarter(axis):
        return y * 2 + (1 - x) if axis == 0 else (1 - y) * 2 + x

    def side_landed(axis, way, k):
        origin = z - (1 - 2 * way) * k
        ref = spot(origin, side_quarter(axis), 0, piece)
        return remote(ref, ref, xsend.at[axis, way, k], xrecv.at[axis, way, k], beside[axis])

    def corner(axis, way, k):
        origin = z - (1 - 2 * way) * k
        ref = spot(origin, side_quarter(axis), axis * (piece // 2), piece // 2)
        return remote(
            ref, ref, dsend.at[axis, way, k], drecv.at[axis, way, k], beside[1 - axis]
        )

    def corner_landed(axis, way, k):
        origin = z - (1 - 2 * way) * k
        ref = spot(origin, (1 - y) * 2 + (1 - x), axis * (piece // 2), piece // 2)
        return remote(
            ref, ref, dsend.at[axis, way, k], drecv.at[axis, way, k], beside[1 - axis]
        )

    def spread(k):
        for way in range(2):
            @pl.when(has(way, k))
            def _():
                landed(way, k).wait_recv()
                if k + 1 < seq:
                    @pl.when(sends(way, k + 1))
                    def _():
                        hop(way, k + 1).start()
                side(0, way, k).start()
                side(1, way, k).start()

    def corners(k):
        for way in range(2):
            @pl.when(has(way, k))
            def _():
                for axis in range(2):
                    side_landed(axis, way, k).wait_recv()
                    corner(axis, way, k).start()

    def settle(k):
        for way in range(2):
            @pl.when(sends(way, k))
            def _():
                hop(way, k).wait_send()

            @pl.when(has(way, k))
            def _():
                for axis in range(2):
                    side(axis, way, k).wait_send()
                    corner(axis, way, k).wait_send()
                    corner_landed(axis, way, k).wait_recv()

    def block(buffer, rank, start, size):
        return buffer.at[pl.ds(pl.multiple_of(rank * rows + start, 16), size)]

    def columns(rank):
        return pl.ds(pl.multiple_of(rank * wide, wide), wide)

    tensors = ((kt, ki, kb), (vt, vi, vb), (qt, qi, qb))

    def inward(o, n):
        peer = ahead(o)
        out = []
        for part, (source, start, size) in enumerate(
            ((tensors[n][0], 0, text), (tensors[n][1], text, image))
        ):
            out.append((
                source.at[0, :, columns(peer)],
                block(tensors[n][2], me, start, size),
                send.at[o, 2 * n + part],
                recv.at[o, 2 * n + part],
                place(peer),
            ))
        return out

    def near(args):
        return pltpu.make_async_copy(args[0], args[1], args[3])

    def scatter(n):
        for i in range(1, count):
            for a in inward(turn(i), n):
                remote(*a).start()

    row = lax.broadcasted_iota(jnp.int32, (rows, dim), 0)

    def take(buffer, rank, text_gain, image_gain):
        gain = jnp.where(row < text, text_gain[...], image_gain[...])
        at = pl.ds(pl.multiple_of(rank * rows, 16), rows)
        for h in range(heads):
            cols = slice(h * dim, (h + 1) * dim)
            buffer[at, cols] = norm_block(buffer[at, cols], gain)

    def outward(o):
        source = behind(o)
        home = source % cores
        return [
            (block(ob, source, 0, text), text_out.at[0, :, columns(me)],
             osend.at[o, 0], orecv.at[o, 0], place(source)),
            (block(ob, source, text, image),
             pair.at[pl.ds(pl.multiple_of(home * image, 16), image), columns(me)],
             osend.at[o, 1], orecv.at[o, 1], place(source)),
        ]

    bias = jnp.where(key_place[...] < length[0], 0.0, -1e30).astype(jnp.float32)

    def work(o):
        source = behind(o)
        take(qb, source, gain_qt, gain_qi)
        at = pl.ds(pl.multiple_of(source * rows, 16), rows)
        for h in range(heads):
            cols = slice(h * dim, (h + 1) * dim)
            scores = lax.dot_general(
                qb[at, cols], kb[:, cols], (((1,), (1,)), ((), ())),
                preferred_element_type=jnp.float32,
            ) * factor + bias
            powers = jnp.exp(scores - jnp.max(scores, axis=1, keepdims=True))
            scale = 1.0 / jnp.sum(powers, axis=1, keepdims=True)
            weights = (powers * scale).astype(jnp.bfloat16)
            ob[at, cols] = jnp.dot(
                weights, vb[:, cols], preferred_element_type=jnp.float32
            ).astype(jnp.bfloat16)

    def wait_recv(o, n):
        for a in inward(o, n):
            remote(*a).wait_recv()

    for n in range(3):
        for a in inward(0, n):
            near(a).start()
    pl.semaphore_wait(barrier, total)
    for way in range(2):
        @pl.when(sends(way, 1))
        def _():
            hop(way, 1).start()
    scatter(0)
    for c in local_copies:
        c.start()
    for n in range(3):
        for a in inward(0, n):
            near(a).wait()
    take(kb, me, gain_kt, gain_ki)
    spread(1)
    scatter(1)

    def keys(i, carry):
        o = turn(i)
        wait_recv(o, 0)
        take(kb, behind(o), gain_kt, gain_ki)
        return carry

    if seq > 2:
        spread(2)
    scatter(2)
    lax.fori_loop(1, count, keys, 0)

    def values(o, carry):
        wait_recv(o, 1)
        return carry

    lax.fori_loop(1, count, values, 0)

    for k in range(3, seq):
        spread(k)
    corners(1)
    work(0)
    for a in outward(0):
        near(a).start()
    for k in range(2, seq - 1):
        corners(k)

    def queries(i, carry):
        o = turn(i)
        wait_recv(o, 2)
        work(o)
        for a in outward(o):
            remote(*a).start()
        return carry

    lax.fori_loop(1, count, queries, 0)
    if seq > 2:
        corners(seq - 1)

    mine = pl.ds(pl.multiple_of(core * image, 16), image)
    theirs = pl.ds(pl.multiple_of(other * image, 16), image)

    def share(o):
        ref = pair.at[mine, columns(ahead(o))]
        return remote(ref, ref, fsend.at[o], frecv.at[o], {"tp": other})

    def shared(o):
        ref = pair.at[theirs, columns(
            lax.rem(z + o // cores, seq) * cores + lax.rem(other + o % cores, cores)
        )]
        return remote(ref, ref, fsend.at[o], frecv.at[o], {"tp": other})

    for a in outward(0):
        near(a).wait()
    share(0).start()
    for c in local_copies:
        c.wait()
    table_rows = table.shape[0]
    selector = lax.broadcasted_iota(jnp.int32, (16, table_rows), 1) == stratum[0]

    def homes(i, carry):
        o = turn(i)
        for a in outward(o):
            src = a[0]
            where = ahead(o)
            dst = (
                text_out.at[0, :, columns(where)]
                if src.shape[0] == text
                else pair.at[mine, columns(where)]
            )
            remote(dst, dst, a[2], a[3], a[4]).wait_recv()
        share(o).start()
        return carry

    lax.fori_loop(1, count, homes, 0)

    def ends(o, carry):
        share(o).wait_send()
        shared(o).wait_recv()
        return carry

    lax.fori_loop(0, count, ends, 0)
    for k in range(1, seq):
        settle(k)

    tiles = half // tile

    def cross(j):
        cols = slice(j * tile, (j + 1) * tile)
        return remote(
            out.at[:, cols], into.at[:, cols], psend.at[j], precv.at[j], {"tp": other}
        )

    for j in range(tiles):
        cols = slice(j * tile, (j + 1) * tile)
        acc[:, cols] = jnp.dot(pair[...], wb[:, cols], preferred_element_type=jnp.float32)
        out[:, cols] = acc[theirs, cols].astype(jnp.bfloat16)
        cross(j).start()

    def finish(branch, base, size):
        cols = pl.ds(pl.multiple_of(base, 128), size)
        gate = jnp.dot(
            selector.astype(jnp.bfloat16), table[:, cols], preferred_element_type=jnp.float32
        )[0:1]
        combined = state[0, :, cols].astype(jnp.float32) + gate * branch
        velocity[0, :, cols] = combined.astype(jnp.bfloat16)
        error = combined - target[0, :, cols].astype(jnp.float32)
        squares = error * error
        lanes = squares[:, 0:128]
        for k in range(1, size // 128):
            lanes = lanes + squares[:, k * 128 : (k + 1) * 128]
        return jnp.sum(lanes, axis=0, keepdims=True)

    partial = jnp.zeros((1, 128), jnp.float32)
    for j in range(tiles):
        partial += finish(
            acc[mine, j * tile : (j + 1) * tile], core * half + j * tile, tile
        )
    for j in range(tiles):
        cross(j).wait_recv()
        partial += finish(
            into[:, j * tile : (j + 1) * tile].astype(jnp.float32), other * half + j * tile, tile
        )
    leave = pltpu.make_async_copy(velocity, velocity_out, lsem.at[4])
    leave.start()
    terms[0] = jnp.broadcast_to(partial, terms.shape[1:])

    def tell(o):
        return remote(
            terms.at[0], terms.at[o], tsend.at[o], trecv.at[o],
            member(lax.rem(group + o, total)),
        )

    for o in range(1, total):
        tell(o).start()
    for j in range(tiles):
        cross(j).wait_send()

    def drain(o, carry):
        for n in range(3):
            for a in inward(o, n):
                remote(*a).wait_send()
        for a in outward(o):
            remote(*a).wait_send()
        return carry

    lax.fori_loop(1, count, drain, 0)
    for o in range(1, total):
        tell(o).wait()
    leave.wait()
    whole = jnp.sum(jnp.sum(terms[...], axis=0)[0:1])
    loss[0] = whole / (image * velocity.shape[2] * total)


def fast(
    query_image,
    key_image,
    value_image,
    query_text,
    key_text,
    value_text,
    image_query_gain,
    image_key_gain,
    text_query_gain,
    text_key_gain,
    text_length,
    strata,
    image_state,
    target,
    out_weight,
    gate_table,
):
    image = query_image.shape[1]
    text = query_text.shape[1]
    rows = image + text
    attn = query_image.shape[2]
    dim = image_query_gain.shape[0]
    width = gate_table.shape[1]
    seq, cores, dp = (lax.axis_size(n) for n in ("seq", "tp", "dp"))
    sizes = (seq, dp, cores)
    count = seq * cores
    total = seq * dp * cores
    wide = attn // count
    half = width // cores
    tile = half // 3 if half % 384 == 0 else half
    key_index = np.arange(count * rows, dtype=np.int32)
    within = key_index % rows
    key_place = np.where(within < text, key_index // rows * text + within, -1)[None, :]
    dma = pltpu.SemaphoreType.DMA
    bf16 = jnp.bfloat16
    smem = pl.BlockSpec(memory_space=pltpu.SMEM)
    return pl.pallas_call(
        functools.partial(whole_kernel, sizes, dim ** (-0.5), tile),
        out_shape=(
            jax.ShapeDtypeStruct((1, image, width), bf16),
            jax.ShapeDtypeStruct((1, text, attn), bf16),
            jax.ShapeDtypeStruct((1,), jnp.float32),
        ),
        in_specs=[ANY] * 10 + [VMEM] * 5 + [smem] * 2,
        out_specs=(ANY, VMEM, smem),
        scratch_shapes=[pltpu.VMEM((1, image, width), bf16)]
        + [pltpu.VMEM((count * rows, wide), bf16)] * 4
        + [
            pltpu.VMEM((cores * image, attn), bf16),
            pltpu.VMEM((attn, half), bf16),
            pltpu.VMEM((1, image, width), bf16),
            pltpu.VMEM((1, image, width), bf16),
            pltpu.VMEM(gate_table.shape, bf16),
            pltpu.VMEM((cores * image, half), jnp.float32),
            pltpu.VMEM((image, half), bf16),
            pltpu.VMEM((image, half), bf16),
            pltpu.VMEM((total, 8, 128), jnp.float32),
            dma((count, 6)), dma((count, 6)), dma((count, 2)), dma((count, 2)),
            dma((count,)), dma((count,)),
            dma((2, seq)), dma((2, seq)), dma((2, 2, seq)), dma((2, 2, seq)),
            dma((2, 2, seq)), dma((2, 2, seq)),
            dma((5,)), dma((half // tile,)), dma((half // tile,)), dma((total,)), dma((total,)),
        ],
        compiler_params=pltpu.CompilerParams(
            collective_id=0, has_side_effects=True, vmem_limit_bytes=60 * 2**20
        ),
    )(
        query_text, query_image, key_text, key_image, value_text, value_image,
        out_weight, image_state, target, gate_table,
        image_query_gain[None], image_key_gain[None], text_query_gain[None], text_key_gain[None],
        jnp.asarray(key_place, jnp.int32), text_length, strata,
    )


def solution(mesh):
    def body(*operands):
        samples, image, attn = operands[0].shape
        heads = attn // operands[6].shape[0]
        shape = dict(mesh.shape)
        fits = (
            samples == 1
            and shape["tp"] == 2
            and heads % (shape["seq"] * shape["tp"]) == 0
            and shape["grp"] == 2
            and shape["dp"] == 2
            and operands[14].shape[0] % 128 == 0
        )
        return fast(*operands) if fits else local(*operands)

    placed = (
        P(("grp", "dp"), ("seq", "tp"), None),
        P(("grp", "dp"), ("seq", "tp"), None),
        P(("grp", "dp"), ("seq", "tp"), None),
        P(("grp", "dp"), ("seq", "tp"), None),
        P(("grp", "dp"), ("seq", "tp"), None),
        P(("grp", "dp"), ("seq", "tp"), None),
        P(),
        P(),
        P(),
        P(),
        P(("grp", "dp")),
        P(("grp", "dp")),
        P(("grp", "dp"), ("seq", "tp"), None),
        P(("grp", "dp"), ("seq", "tp"), None),
        P("seq", "tp"),
        P(),
    )
    return jax.shard_map(
        body,
        mesh=mesh,
        in_specs=placed,
        out_specs=(
            P(("grp", "dp"), ("seq", "tp"), None),
            P(("grp", "dp"), ("seq", "tp"), None),
            P("grp"),
        ),
        check_vma=False,
    )
```
